32 devices in a mesh: pert: 2 (over y), band: 16 (over z, x, core).
Axes of the slice: x: 2, y: 2, z: 4, core: 2. Of those that a mesh axis runs over, the one named last changes fastest.
Arguments:
- response: bfloat16 [1024, 12288], P('pert', 'band'), parts along dimension 0, may hold values from -6 to 6
- orbitals: bfloat16 [512, 12288], P(None, 'band'), may hold values from -6 to 6
- projectors: bfloat16 [2048, 12288], P(None, 'band'), may hold values from -6 to 6
- potential: float32 [12288], P('band'), may hold values from -1 to 1
- perturbing: float32 [24576], P(('pert', 'band')), parts along dimension 0, may hold values from -6 to 6
- energies: float32 [512], replicated, may hold values from -1 to -0.2
- window_start: int32 [512], replicated, may hold values from 0 to 31, as said below
- block_count: int32 [512], replicated, may hold values from 1 to 9, as said below
Outputs:
- updated_response: bfloat16 [1024, 12288], P('pert', 'band'), parts along dimension 0
- residual: bfloat16 [1024, 12288], P('pert', 'band'), parts along dimension 0
The draws below stay inside these ranges and needn't reach their ends.
There are 2 independent parts, one for each index of `pert`. The reference program is written for one: setup_inputs(seed, part) draws one part's arguments, and reference() takes and returns one part's arrays. A program takes and returns all parts, laid end to end along the dimension named above; an argument that names none is the same for every part. Nothing has to cross between parts.
Inputs may be any that keep to these rules, and one draw needn't show every extreme that they name: `window_start`: band n lies in block n // 16. Each band's window contains its own block and starts at most 4 blocks below it. `block_count`: each band's window ends at most 4 blocks above its own block and never past block 31.
All inputs are finite; a program needn't handle non-finite values.
Results may differ from the reference program's by a relative error of at most 0.0041.
Values may be sent and summed in bfloat16 or wider, within the bound.
A program may use at most 128 MiB of HBM per device.

```python
import math
import jax
import jax.numpy as jnp

GY = 8
GZ = 16
NOCC = 2048
NBW = 512
NBLK = 32
REACH = 4
GX = 96
CELLS = 12288
BLK = 16


def window_parts(key):
    base_key = jax.random.fold_in(key, 11)
    lower_reach = jax.random.randint(jax.random.fold_in(base_key, 1), (NBW,), 0, REACH + 1)
    upper_reach = jax.random.randint(jax.random.fold_in(base_key, 2), (NBW,), 0, REACH + 1)
    band_index = jnp.arange(NBW, dtype=jnp.int32)
    own_block = band_index // BLK
    widest = band_index == NBLK // 2 * BLK
    lower_reach = jnp.where(widest, REACH, lower_reach)
    upper_reach = jnp.where(widest, REACH, upper_reach)
    final_band = band_index == NBW - 1
    lower_reach = jnp.where(final_band, 0, lower_reach)
    first_block = jnp.maximum(own_block - lower_reach, 0)
    last_block = jnp.minimum(own_block + upper_reach, NBLK - 1)
    return (first_block.astype(jnp.int32), (last_block - first_block + 1).astype(jnp.int32))


def draw_window_start(key, part):
    return window_parts(key)[0]


def draw_block_count(key, part):
    return window_parts(key)[1]


def level_of(stream_key, extent, cuts, smallest, largest):
    def one(dim, blocks):
        draws = jax.random.uniform(jax.random.fold_in(jax.random.fold_in(stream_key, 6), dim), (blocks,), jnp.float32, smallest / len(cuts), largest / len(cuts))
        return jnp.repeat(jnp.exp(draws), extent[dim] // blocks).reshape((-1,) + (1,) * (len(extent) - dim - 1))

    gain = one(*cuts[0])
    for cut in cuts[1:]:
        gain = gain * one(*cut)
    return gain


def centred(key, dims, deviation, limit, shards=(), held_as=jnp.bfloat16):
    array = deviation * jax.random.normal(key, dims, jnp.float32)
    if shards:
        array = array * level_of(key, dims, shards, -0.22, 0.18)
    return jnp.clip(array, -limit, limit).astype(held_as)


def setup_inputs(seed: int = 0, part: int = 0) -> dict:
    splits = jax.random.split(jax.random.key(seed), 9)
    part_splits = jax.random.split(jax.random.fold_in(splits[8], part), 9)
    return {
        "response": centred(part_splits[0], (NBW, CELLS), 1.0, 6.0, ((1, 16),)),
        "orbitals": centred(splits[1], (NBW, CELLS), 1.0, 6.0, ((1, 16),)),
        "projectors": centred(splits[2], (NOCC, CELLS), 1.0, 6.0, ((1, 16),)),
        "potential": jnp.clip(jax.random.uniform(splits[3], (CELLS,), jnp.float32, -1.0, 1.0) * level_of(splits[3], (CELLS,), ((0, 16),), -0.4, 0.0), -1.0, 1.0),
        "perturbing": centred(part_splits[4], (CELLS,), 1.0, 6.0, ((0, 16),), jnp.float32),
        "energies": jnp.clip(jax.random.uniform(splits[5], (NBW,), jnp.float32, -1.0, -0.2), -1.0, -0.2),
        "window_start": draw_window_start(jax.random.fold_in(splits[8], 71), part),
        "block_count": draw_block_count(jax.random.fold_in(splits[8], 71), part),
    }


COEFFS = (-5369.0 / 1800.0, 12.0 / 7.0, -15.0 / 56.0, 10.0 / 189.0, -1.0 / 112.0, 2.0 / 1925.0, -1.0 / 16632.0)
KINETIC = 0.125
STEP_SIZE = 0.3

def laplacian(grid_field):
    result = 3.0 * COEFFS[0] * grid_field
    for axis_number in (1, 2, 3):
        for offset in range(1, 7):
            result = result + COEFFS[offset] * (jnp.roll(grid_field, offset, axis_number) + jnp.roll(grid_field, -offset, axis_number))
    return result

def reference(response, orbitals, projectors, potential, perturbing, energies, window_start, block_count):
    cells = GX * GY * GZ
    ace_scale = 1.0 / math.sqrt(cells * NOCC)
    window_scale = 1.0 / math.sqrt(cells * NBW)
    response_wide = response.astype(jnp.float32)
    kinetic = -KINETIC * laplacian(response_wide.reshape(NBW, GX, GY, GZ)).reshape(NBW, cells)
    ace_intersection = (jnp.dot(response, projectors.T, preferred_element_type=jnp.float32) * ace_scale).astype(jnp.bfloat16)
    ace_term = -jnp.dot(ace_intersection, projectors, preferred_element_type=jnp.float32)
    applied = kinetic + potential[None, :] * response_wide + ace_term - energies[:, None] * response_wide
    orbitals_wide = orbitals.astype(jnp.float32)
    unprojected = -(perturbing[None, :] * orbitals_wide) - applied
    unprojected_low = unprojected.astype(jnp.bfloat16)
    intersections = (jnp.dot(unprojected_low, orbitals.T, preferred_element_type=jnp.float32) * window_scale).astype(jnp.bfloat16)
    block_ids = jnp.arange(NBW, dtype=jnp.int32) // (NBW // NBLK)
    lowest = window_start[:, None]
    highest = window_start[:, None] + block_count[:, None] - 1
    inside = (block_ids[None, :] >= lowest) & (block_ids[None, :] <= highest)
    intersections = jnp.where(inside, intersections, jnp.zeros_like(intersections))
    residual_wide = unprojected - jnp.dot(intersections, orbitals, preferred_element_type=jnp.float32)
    updated_response = (response_wide + STEP_SIZE * residual_wide).astype(jnp.bfloat16)
    return (updated_response, residual_wide.astype(jnp.bfloat16))
```

```python
import functools
import itertools
import math

import jax
import jax.numpy as jnp
import numpy as np
from jax import lax
from jax.experimental import pallas as pl
from jax.experimental.pallas import tpu as pltpu
from jax.sharding import PartitionSpec as P

GY = 8
GZ = 16
NBLK = 32
REACH = 4


COEFFS = (
    -5369.0 / 1800.0,
    12.0 / 7.0,
    -15.0 / 56.0,
    10.0 / 189.0,
    -1.0 / 112.0,
    2.0 / 1925.0,
    -1.0 / 16632.0,
)
KINETIC = 0.125
STEP_SIZE = 0.3
HALO = 6
NT = (((1,), (1,)), ((), ()))
GROUPS = 4
CHUNK = 1024
WINDOW = 256
ROWS = 32
TILE = 128
PIECE = 16
LEVELS = 4
INWARD, MIDDLE, OUTWARD, ACROSS, SHARE, REST, KEPT, CORE, WHOLE, KINDS = range(10)
WAYS = ("x", "x", "x", "z", "x", "x", "x", "w")
ORDER = (
    ("B", "hs", 0), ("B", "p", 0), ("B", "p", 1), ("B", "p", 4), ("E", "1", 0), ("M", "1", 0),
    ("B", "p", 5), ("E", "1", 1), ("E", "1", 2), ("E", "1", 3), ("M", "1", 1), ("M", "1", 2),
    ("B", "mask", 0), ("E", "1", 4), ("M", "1", 4), ("B", "loc", 0), ("B", "hs", 1),
    ("E", "2", 0), ("E", "1", 5), ("E", "1", 6), ("M", "1", 5), ("M", "2", 0), ("M", "1", 6),
    ("B", "ht", 0), ("B", "loc", 1), ("E", "2", 1), ("M", "2", 1), ("B", "loc", 2), ("E", "2", 2),
    ("E", "1", 7), ("M", "2", 2), ("M", "2", 3), ("M", "1", 7), ("B", "loc", 3), ("E", "2", 4),
    ("M", "2", 4), ("M", "3", 0), ("M", "3", 3), ("M", "3", 1), ("B", "ht", 1), ("B", "hs", 2),
    ("E", "2", 5), ("E", "2", 6), ("M", "2", 5), ("M", "3", 2), ("M", "2", 6), ("M", "4", 0),
    ("M", "4", 3), ("B", "hs", 3), ("E", "2", 7), ("E", "5", 0), ("M", "4", 1), ("M", "2", 7),
    ("M", "3", 4), ("M", "4", 2), ("M", "5", 3), ("M", "3", 5), ("B", "ht", 2), ("E", "5", 1),
    ("E", "5", 2), ("E", "3", 7), ("M", "5", 0), ("M", "7", 3), ("M", "3", 6), ("M", "7", 0),
    ("M", "4", 4), ("M", "4", 5), ("B", "ht", 3), ("E", "6", 3), ("E", "6", 0), ("E", "7", 3),
    ("E", "5", 4), ("E", "7", 0), ("E", "6", 1), ("E", "5", 5), ("E", "7", 1), ("M", "5", 1),
    ("M", "4", 6), ("M", "3", 7), ("M", "7", 1), ("B", "app", 0), ("E", "6", 2), ("E", "5", 6),
    ("E", "6", 4), ("E", "7", 2), ("M", "5", 2), ("M", "5", 4), ("M", "7", 2), ("B", "app", 1),
    ("E", "7", 4), ("E", "6", 5), ("E", "4", 7), ("M", "7", 4), ("M", "5", 5), ("M", "5", 6),
    ("M", "7", 5), ("M", "7", 6), ("M", "4", 7), ("B", "cmb", 0), ("E", "6", 6), ("E", "7", 5),
    ("M", "7", 7), ("B", "app", 2), ("E", "7", 6), ("E", "7", 7), ("B", "app", 3),
    ("B", "cmb", 1), ("B", "fin", 0), ("B", "cmb", 2), ("B", "cmb", 3), ("B", "fin", 1),
    ("B", "fin", 2), ("B", "fin", 3),
)


CONTRACT_CELLS = (((1,), (1,)), ((), ()))


def padded_2(cells, sides, width):
    for axis, dim in sides:
        count = lax.axis_size(axis)
        head = lax.slice_in_dim(cells, 0, width, axis=dim)
        tail = lax.slice_in_dim(cells, cells.shape[dim] - width, cells.shape[dim], axis=dim)
        cells = jnp.concatenate(
            [
                lax.ppermute(tail, axis, [(i, (i + 1) % count) for i in range(count)]),
                cells,
                lax.ppermute(head, axis, [((i + 1) % count, i) for i in range(count)]),
            ],
            axis=dim,
        )
    return cells


def slab_laplacian(padded, depth):
    centre = padded[:, 6 : 6 + depth]
    result = 3.0 * COEFFS[0] * centre
    for offset in range(1, 7):
        result = result + COEFFS[offset] * (
            padded[:, 6 + offset : 6 + offset + depth] + padded[:, 6 - offset : 6 - offset + depth]
        )
    for axis_number in (2, 3):
        for offset in range(1, 7):
            result = result + COEFFS[offset] * (
                jnp.roll(centre, offset, axis_number) + jnp.roll(centre, -offset, axis_number)
            )
    return result


def plain_shards(
    response, orbitals, projectors, potential, perturbing, energies, window_start, block_count
):
    band_rows = response.shape[0]
    local_cells = response.shape[1]
    devices = lax.axis_size("band")
    cells = local_cells * devices
    plane = GY * GZ
    depth = local_cells // plane
    ace_scale = 1.0 / math.sqrt(cells * projectors.shape[0])
    window_scale = 1.0 / math.sqrt(cells * band_rows)
    padded = padded_2(response.reshape(band_rows, depth, plane), (("band", 1),), 6)
    padded_wide = padded.astype(jnp.float32).reshape(band_rows, depth + 12, GY, GZ)
    kinetic = -KINETIC * slab_laplacian(padded_wide, depth).reshape(band_rows, local_cells)
    response_wide = response.astype(jnp.float32)
    picked = response
    share = lax.psum_scatter(
        lax.dot_general(picked, projectors, CONTRACT_CELLS, preferred_element_type=jnp.float32),
        "band",
        scatter_dimension=0,
        tiled=True,
    )
    ace_intersection = lax.all_gather(
        (share * ace_scale).astype(jnp.bfloat16), "band", axis=0, tiled=True
    )
    ace_term = -jnp.dot(ace_intersection, projectors, preferred_element_type=jnp.float32)
    applied = (
        kinetic + potential[None, :] * response_wide + ace_term - energies[:, None] * response_wide
    )
    orbitals_wide = orbitals.astype(jnp.float32)
    unprojected = -(perturbing[None, :] * orbitals_wide) - applied
    unprojected_low = unprojected.astype(jnp.bfloat16)
    picked = unprojected_low
    window_share = lax.psum_scatter(
        lax.dot_general(picked, orbitals, CONTRACT_CELLS, preferred_element_type=jnp.float32),
        "band",
        scatter_dimension=0,
        tiled=True,
    )
    window_intersection = lax.all_gather(
        (window_share * window_scale).astype(jnp.bfloat16), "band", axis=0, tiled=True
    )
    block_ids = jnp.arange(band_rows, dtype=jnp.int32) // (band_rows // NBLK)
    lowest = window_start[:, None]
    highest = window_start[:, None] + block_count[:, None] - 1
    inside = (block_ids[None, :] >= lowest) & (block_ids[None, :] <= highest)
    window_intersection = jnp.where(
        inside, window_intersection, jnp.zeros_like(window_intersection)
    )
    residual_wide = unprojected - jnp.dot(
        window_intersection, orbitals, preferred_element_type=jnp.float32
    )
    updated_response = (response_wide + STEP_SIZE * residual_wide).astype(jnp.bfloat16)
    return (updated_response, residual_wide.astype(jnp.bfloat16))


def plane_operator():
    plane = GY * GZ
    op = np.zeros((plane, plane), np.float64)
    for y in range(GY):
        for z in range(GZ):
            out = y * GZ + z
            op[out, out] += 3.0 * COEFFS[0]
            for k in range(1, HALO + 1):
                for sign in (-k, k):
                    op[((y + sign) % GY) * GZ + z, out] += COEFFS[k]
                    op[y * GZ + (z + sign) % GZ, out] += COEFFS[k]
    return (KINETIC * op).astype(np.float32)


def kernel(
    count, ace_scale, window_scale,
    resp_hbm, orb_hbm, proj_hbm, pot, pert, energies, first, blocks, op_hi, op_lo,
    wide_hbm,
    resp, orb, proj, halo_l, halo_r, unp, acc, c_send, c_recv, e_send, e_recv, z_send, z_recv,
    x_send, x_recv, full, w_sum, w_send, w_recv, w_full, inside, energy, wide,
    send_sem, recv_sem, halo_send, halo_recv, load_sem, ws_send, ws_recv, wg_send, wg_recv, out_sem,
):
    rows, cells = resp.shape
    plane = GY * GZ
    depth = cells // plane
    height = rows // GROUPS
    half, quarter = height // 2, height // 4
    pieces = proj.shape[0] // CHUNK
    total = GROUPS * pieces
    block = rows // NBLK
    reach = REACH * block

    me = lax.axis_index("band")
    core = me % 2
    across = (me // 2) % 2
    level = me // 4
    edge = (level == 0) | (level == LEVELS - 1)
    mid = jnp.logical_not(edge)
    upper = level // 2
    left, right = (me + count - 1) % count, (me + 1) % count
    core_peer = me + 1 - 2 * core
    x_peer = me + 2 - 4 * across
    e_peer = me + 4 - 8 * (level % 2)
    m_peer = (LEVELS - 1 - level) * 4 + me % 4
    everyone = [(me + k) % count for k in range(1, count)]

    def remote(src, dst, send, recv, device):
        return pltpu.make_async_remote_copy(
            src_ref=src, dst_ref=dst, send_sem=send, recv_sem=recv,
            device_id={"band": device}, device_id_type=pl.DeviceIdType.MESH,
        )

    loads = [pltpu.make_async_copy(resp_hbm, resp, load_sem.at[0])]
    for j in range(pieces):
        at = pl.ds(j * CHUNK, CHUNK)
        loads.append(
            pltpu.make_async_copy(proj_hbm.at[at, :], proj.at[at, :], load_sem.at[1 + j])
        )
    loads.append(pltpu.make_async_copy(orb_hbm, orb, load_sem.at[1 + pieces]))
    for load in loads:
        load.start()

    barrier = pltpu.get_barrier_semaphore()
    for device in everyone:
        pl.semaphore_signal(
            barrier, inc=1, device_id={"band": device}, device_id_type=pl.DeviceIdType.MESH
        )

    core_row = pl.multiple_of(core * half, half)
    other_row = pl.multiple_of((1 - core) * half, half)

    def span(g):
        return slice(g * height, (g + 1) * height)

    halos = []
    for g in range(GROUPS):
        at = pl.ds(g * height, height)
        halos.append((
            remote(
                resp.at[at, :], halo_l.at[at, :], halo_send.at[g, 0], halo_recv.at[g, 0], right
            ),
            remote(
                resp.at[at, :], halo_r.at[at, :], halo_send.at[g, 1], halo_recv.at[g, 1], left
            ),
        ))

    def halo_start(g):
        for copy in halos[g]:
            copy.start()

    def rest_rows(offset, size):
        return pl.ds(pl.multiple_of(core_row + offset, PIECE), size)

    sixteenth = half // LEVELS
    z_ring = [(level + k) % LEVELS for k in range(1, LEVELS)]

    def copy_of(q, kind):
        sems = (send_sem.at[q, kind], recv_sem.at[q, kind])
        way = WAYS[q]
        if kind == CORE:
            return remote(c_send.at[q], c_recv.at[q], *sems, core_peer)
        if kind == WHOLE:
            whole = full.at[q, pl.ds(core_row, half), :]
            return remote(whole, whole, *sems, core_peer)
        if way == "w":
            if kind == ACROSS:
                at = pl.ds(0, sixteenth)
                return remote(x_send.at[q, at, :], x_recv.at[q, at, :], *sems, x_peer)
            k = kind % 4
            device = z_ring[k] * 4 + me % 4
            if kind < SHARE:
                there = pl.ds(pl.multiple_of(z_ring[k] * sixteenth, sixteenth), sixteenth)
                here = pl.ds(k * sixteenth, sixteenth)
                return remote(e_send.at[q, there, :], e_recv.at[q, here, :], *sems, device)
            mine = full.at[q, rest_rows(level * sixteenth, sixteenth), :]
            return remote(mine, mine, *sems, device)
        along = way == "z"
        own = (upper if along else across) * quarter
        if kind == INWARD:
            if along:
                return remote(e_send.at[q], e_recv.at[q], *sems, e_peer)
            small = pl.ds(0, quarter)
            return remote(e_send.at[q, small, :], e_recv.at[q, small, :], *sems, e_peer)
        if kind == MIDDLE:
            return remote(z_send.at[q], z_recv.at[q], *sems, m_peer)
        if kind == ACROSS:
            return remote(x_send.at[q], x_recv.at[q], *sems, x_peer)
        mine = full.at[q, rest_rows(own, quarter), :]
        if kind == SHARE:
            return remote(mine, mine, *sems, m_peer if along else x_peer)
        if kind == OUTWARD:
            return remote(mine, mine, *sems, e_peer)
        rest = full.at[q, rest_rows((1 - upper) * quarter, quarter), :]
        return remote(rest, rest, *sems, e_peer)

    sent = {}

    def start(role, q, *kinds):
        for kind in kinds:
            copy_of(q, kind).start()
            sent.setdefault(role, []).append((q, kind))

    def wait(q, *kinds):
        for kind in kinds:
            copy_of(q, kind).wait_recv()

    low, wider = jnp.bfloat16, jnp.float32

    def partials(pair, h):
        if pair == 0:
            loads[1 + h].wait()
        value = lax.dot_general(
            resp[pair * 2 * height : (pair + 1) * 2 * height, :],
            proj[h * CHUNK : (h + 1) * CHUNK, :], NT, preferred_element_type=wider,
        )
        for k in range(2):
            q = (2 * pair + k) * pieces + h
            acc[q] = value[k * height : (k + 1) * height]
            c_send[q] = acc[q, pl.ds(other_row, half), :].astype(low)
            start("B", q, CORE)

    def core_sum(q, offset, size):
        if not isinstance(offset, int):
            offset = pl.multiple_of(offset, PIECE)
        at = pl.multiple_of(core_row + offset, PIECE)
        return acc[q, pl.ds(at, size), :] + c_recv[q, pl.ds(offset, size), :].astype(wider)

    def held(q, offset):
        return acc.at[q, rest_rows(offset, quarter), :]

    def along_z(role, s, q):
        mine, rest = upper * quarter, (1 - upper) * quarter
        if s == 1:
            wait(q, CORE)
            e_send[q] = core_sum(q, 0, half).astype(low)
            start(role, q, INWARD)
        if s == 2:
            wait(q, CORE, INWARD)
            at = pl.ds(pl.multiple_of(rest, quarter), quarter)
            z_send[q] = (core_sum(q, rest, quarter) + e_recv[q, at, :].astype(wider)).astype(low)
            start(role, q, MIDDLE)
            at = pl.ds(pl.multiple_of(mine, quarter), quarter)
            held(q, mine)[...] = core_sum(q, mine, quarter) + e_recv[q, at, :].astype(wider)
        if s == 3:
            wait(q, MIDDLE)
            value = held(q, mine)[...] + z_recv[q].astype(wider)
            x_send[q] = value.astype(low)
            start(role, q, ACROSS)
            held(q, mine)[...] = value
        if s == 4:
            wait(q, ACROSS)
            value = held(q, mine)[...] + x_recv[q].astype(wider)
            full[q, rest_rows(mine, quarter), :] = (value * ace_scale).astype(low)
            start(role, q, SHARE, OUTWARD)
        if s == 5:
            wait(q, SHARE)
            start(role, q, REST, WHOLE)
        if s == 6:
            wait(q, OUTWARD, REST)
            start(role, q, WHOLE)

    def along_x(role, s, q):
        mine, rest = across * quarter, (1 - across) * quarter
        if s == 1:
            wait(q, CORE)
            x_send[q] = core_sum(q, rest, quarter).astype(low)
            start(role, q, ACROSS)
        if s == 2:
            wait(q, ACROSS)
            value = core_sum(q, mine, quarter) + x_recv[q].astype(wider)
            if role == "E":
                e_send[q, :quarter, :] = value.astype(low)
                start(role, q, INWARD)
            else:
                held(q, mine)[...] = value
        if s == 3:
            wait(q, INWARD)
            value = held(q, mine)[...] + e_recv[q, :quarter, :].astype(wider)
            z_send[q] = value.astype(low)
            start(role, q, MIDDLE)
            held(q, mine)[...] = value
        if s == 4:
            wait(q, MIDDLE)
            value = held(q, mine)[...] + z_recv[q].astype(wider)
            full[q, rest_rows(mine, quarter), :] = (value * ace_scale).astype(low)
            start(role, q, OUTWARD, SHARE)
        if s == 5 and role == "E":
            wait(q, OUTWARD)
            start(role, q, SHARE)
        if s == 5 and role == "M":
            wait(q, SHARE)
            start(role, q, WHOLE)
        if s == 6:
            wait(q, SHARE)
            start(role, q, WHOLE)

    def direct(role, s, q):
        if s == 1:
            wait(q, CORE)
            e_send[q] = core_sum(q, 0, half).astype(low)
            start(role, q, 0, 1, 2)
        if s == 2:
            wait(q, 0, 1, 2)
            value = core_sum(q, level * sixteenth, sixteenth)
            for k in range(LEVELS - 1):
                at = slice(k * sixteenth, (k + 1) * sixteenth)
                value = value + e_recv[q, at, :].astype(wider)
            x_send[q, :sixteenth, :] = value.astype(low)
            start(role, q, ACROSS)
            acc[q, rest_rows(level * sixteenth, sixteenth), :] = value
        if s == 3:
            wait(q, ACROSS)
            at = rest_rows(level * sixteenth, sixteenth)
            value = acc[q, at, :] + x_recv[q, :sixteenth, :].astype(wider)
            full[q, at, :] = (value * ace_scale).astype(low)
            start(role, q, 4, 5, 6)
        if s == 4:
            wait(q, 4, 5, 6)
            start(role, q, WHOLE)

    chains = {"z": along_z, "x": along_x, "w": direct}

    def column(ref):
        return jnp.broadcast_to(ref[...].astype(wider), (plane, rows)).T

    def window(g):
        return min(max(g * height - reach, 0), rows - WINDOW)

    def masks():
        begin = column(first)
        end = begin + column(blocks)
        lanes = lax.broadcasted_iota(jnp.int32, (height, TILE), 1).astype(wider)
        for g in range(GROUPS):
            for t in range(WINDOW // TILE):
                ids = jnp.floor((lanes + float(window(g) + t * TILE)) * (1.0 / block))
                keep = (ids >= begin[span(g)]) & (ids < end[span(g)])
                inside[g, t] = jnp.where(keep, 1.0, 0.0)
        energy[...] = column(energies)

    def local_terms(g):
        for p in range(depth):
            cut = resp[span(g), p * plane : (p + 1) * plane]
            unp[span(g), p * plane : (p + 1) * plane] = jnp.dot(
                cut, op_hi[...], preferred_element_type=wider
            ) + jnp.dot(cut, op_lo[...], preferred_element_type=wider)

        @pl.loop(0, height // ROWS)
        def _(i):
            at = pl.ds(pl.multiple_of(g * height + i * ROWS, ROWS), ROWS)
            planes = [resp[at, p * plane : (p + 1) * plane].astype(wider) for p in range(depth)]
            level_of = energy[at, :]
            for p in range(depth):
                cut = slice(p * plane, (p + 1) * plane)
                value = unp[at, cut] + (level_of - pot[cut]) * planes[p]
                value = value - pert[cut] * orb[at, cut].astype(wider)
                for k in range(1, HALO + 1):
                    for q in (p - k, p + k):
                        if 0 <= q < depth:
                            value = value + (KINETIC * COEFFS[k]) * planes[q]
                unp[at, cut] = value

    def halo_terms(g):
        for copy in halos[g]:
            copy.wait_recv()

        @pl.loop(0, height // ROWS)
        def _(i):
            at = pl.ds(pl.multiple_of(g * height + i * ROWS, ROWS), ROWS)
            before = [
                halo_l[at, p * plane : (p + 1) * plane].astype(wider) for p in range(HALO)
            ]
            after = [
                halo_r[at, p * plane : (p + 1) * plane].astype(wider) for p in range(HALO)
            ]
            for p in range(depth):
                value = unp[at, p * plane : (p + 1) * plane]
                for k in range(1, HALO + 1):
                    if p - k < 0:
                        value = value + (KINETIC * COEFFS[k]) * before[HALO + p - k]
                    if p + k >= depth:
                        value = value + (KINETIC * COEFFS[k]) * after[p + k - depth]
                unp[at, p * plane : (p + 1) * plane] = value

    def place(device):
        return pl.ds(pl.multiple_of((device // 2) * PIECE, PIECE), PIECE), device % 2

    def apply(g):
        weights = jnp.concatenate([full[g * pieces + h] for h in range(pieces)], axis=1)
        low_parts = []
        for lo in range(0, cells, WINDOW):
            value = unp[span(g), lo : lo + WINDOW] + jnp.dot(
                weights, proj[:, lo : lo + WINDOW], preferred_element_type=wider
            )
            unp[span(g), lo : lo + WINDOW] = value
            low_parts.append(value.astype(low))
        value = lax.dot_general(
            jnp.concatenate(low_parts, axis=1), orb[window(g) : window(g) + WINDOW, :], NT,
            preferred_element_type=wider,
        )
        for t in range(WINDOW // TILE):
            w_sum[g, t] = value[:, t * TILE : (t + 1) * TILE]
            w_send[g, t] = value[:, t * TILE : (t + 1) * TILE].astype(low)
        for k, device in enumerate(everyone):
            at, t = place(device)
            remote(
                w_send.at[g, t, at, :], w_recv.at[g, k], ws_send.at[g], ws_recv.at[g], device
            ).start()

    def drain(sem, g):
        pltpu.make_async_copy(w_recv.at[g], w_recv.at[g], sem.at[g]).wait()

    def combine(g):
        drain(ws_recv, g)
        at, t = place(me)
        value = w_sum[g, t, at, :]
        for k in range(count - 1):
            value = value + w_recv[g, k].astype(wider)
        w_full[g, t, at, :] = (value * window_scale).astype(low)
        mine = w_full.at[g, t, at, :]
        for device in everyone:
            remote(mine, mine, wg_send.at[g], wg_recv.at[g], device).start()

    outs = [
        pltpu.make_async_copy(wide.at[span(g), :], wide_hbm.at[span(g), :], out_sem.at[g])
        for g in range(GROUPS)
    ]

    def finish(g):
        drain(wg_recv, g)
        weights = jnp.concatenate(
            [
                (w_full[g, t].astype(wider) * inside[g, t]).astype(low)
                for t in range(WINDOW // TILE)
            ],
            axis=1,
        )
        wide[span(g), :] = unp[span(g), :] - jnp.dot(
            weights, orb[window(g) : window(g) + WINDOW, :], preferred_element_type=wider
        )
        outs[g].start()

    def orbitals_ready():
        loads[1 + pieces].wait()
        masks()

    common = {
        "hs": halo_start, "loc": local_terms, "ht": halo_terms,
        "app": apply, "cmb": combine, "fin": finish,
    }

    def perform(role, name, number):
        if name == "p":
            partials(number // (2 * pieces), number % (2 * pieces))
        elif name == "mask":
            orbitals_ready()
        elif name in common:
            common[name](number)
        elif name == "7":
            wait(number, WHOLE)
        else:
            chains[WAYS[number]](role, int(name), number)

    loads[0].wait()
    pl.semaphore_wait(barrier, count - 1)
    for role, run in itertools.groupby(ORDER, key=lambda step: step[0]):
        run = list(run)

        def body():
            for step in run:
                perform(*step)

        if role == "B":
            body()
        else:
            pl.when(edge if role == "E" else mid)(body)

    for copy in outs:
        copy.wait()
    for g in range(GROUPS):
        for copy in halos[g]:
            copy.wait_send()
        drain(ws_send, g)
        drain(wg_send, g)
    for role, condition in (("B", None), ("E", edge), ("M", mid)):
        def body():
            for q, kind in sent[role]:
                copy_of(q, kind).wait_send()

        if condition is None:
            body()
        else:
            pl.when(condition)(body)


def shards(
    response, orbitals, projectors, potential, perturbing, energies, window_start, block_count
):
    rows, local = response.shape
    count = lax.axis_size("band")
    cells = local * count
    pieces = projectors.shape[0] // CHUNK
    total = GROUPS * pieces
    height = rows // GROUPS
    half, quarter = height // 2, height // 4
    op = plane_operator()
    op_hi = jnp.asarray(op).astype(jnp.bfloat16)
    op_lo = (jnp.asarray(op) - op_hi.astype(jnp.float32)).astype(jnp.bfloat16)
    low, wider = jnp.bfloat16, jnp.float32
    tiles = WINDOW // TILE
    vmem = pl.BlockSpec(memory_space=pltpu.VMEM)
    hbm = pl.BlockSpec(memory_space=pl.ANY)
    wide = pl.pallas_call(
        functools.partial(
            kernel, count,
            1.0 / math.sqrt(cells * projectors.shape[0]), 1.0 / math.sqrt(cells * rows),
        ),
        out_shape=jax.ShapeDtypeStruct(response.shape, wider),
        in_specs=[hbm] * 3 + [vmem] * 7,
        out_specs=hbm,
        scratch_shapes=[
            pltpu.VMEM(response.shape, low),
            pltpu.VMEM(orbitals.shape, low),
            pltpu.VMEM(projectors.shape, low),
            pltpu.VMEM(response.shape, low),
            pltpu.VMEM(response.shape, low),
            pltpu.VMEM(response.shape, wider),
            pltpu.VMEM((total, height, CHUNK), wider),
            pltpu.VMEM((total, half, CHUNK), low),
            pltpu.VMEM((total, half, CHUNK), low),
            pltpu.VMEM((total, half, CHUNK), low),
            pltpu.VMEM((total, half, CHUNK), low),
            pltpu.VMEM((total, quarter, CHUNK), low),
            pltpu.VMEM((total, quarter, CHUNK), low),
            pltpu.VMEM((total, quarter, CHUNK), low),
            pltpu.VMEM((total, quarter, CHUNK), low),
            pltpu.VMEM((total, height, CHUNK), low),
            pltpu.VMEM((GROUPS, tiles, height, TILE), wider),
            pltpu.VMEM((GROUPS, tiles, height, TILE), low),
            pltpu.VMEM((GROUPS, count - 1, PIECE, TILE), low),
            pltpu.VMEM((GROUPS, tiles, height, TILE), low),
            pltpu.VMEM((GROUPS, tiles, height, TILE), wider),
            pltpu.VMEM((rows, GY * GZ), wider),
            pltpu.VMEM(response.shape, wider),
            pltpu.SemaphoreType.DMA((total, KINDS)),
            pltpu.SemaphoreType.DMA((total, KINDS)),
            pltpu.SemaphoreType.DMA((GROUPS, 2)),
            pltpu.SemaphoreType.DMA((GROUPS, 2)),
            pltpu.SemaphoreType.DMA((pieces + 2,)),
            pltpu.SemaphoreType.DMA((GROUPS,)),
            pltpu.SemaphoreType.DMA((GROUPS,)),
            pltpu.SemaphoreType.DMA((GROUPS,)),
            pltpu.SemaphoreType.DMA((GROUPS,)),
            pltpu.SemaphoreType.DMA((GROUPS,)),
        ],
        compiler_params=pltpu.CompilerParams(
            collective_id=0, has_side_effects=True, vmem_limit_bytes=56 * 1024 * 1024
        ),
    )(
        response, orbitals, projectors,
        potential, perturbing,
        energies[None, :], window_start[None, :], block_count[None, :],
        op_hi, op_lo,
    )
    updated = response.astype(wider) + STEP_SIZE * wide
    return updated.astype(low), wide.astype(low)


def solution(mesh):
    fits = mesh.shape["band"] == 4 * LEVELS
    in_specs = (
        P("pert", "band"),
        P(None, "band"),
        P(None, "band"),
        P("band"),
        P(("pert", "band")),
        P(),
        P(),
        P(),
    )
    out_specs = (P("pert", "band"), P("pert", "band"))
    return jax.shard_map(
        shards if fits else plain_shards,
        mesh=mesh, in_specs=in_specs, out_specs=out_specs, check_vma=False,
    )
```

```python
import functools
import itertools
import math

import jax
import jax.numpy as jnp
import numpy as np
from jax import lax
from jax.experimental import pallas as pl
from jax.experimental.pallas import tpu as pltpu
from jax.sharding import PartitionSpec as P

GY = 8
GZ = 16
NBLK = 32
REACH = 4


COEFFS = (
    -5369.0 / 1800.0,
    12.0 / 7.0,
    -15.0 / 56.0,
    10.0 / 189.0,
    -1.0 / 112.0,
    2.0 / 1925.0,
    -1.0 / 16632.0,
)
KINETIC = 0.125
STEP_SIZE = 0.3
HALO = 6
NT = (((1,), (1,)), ((), ()))
GROUPS = 4
CHUNK = 1024
WINDOW = 256
ROWS = 32
TILE = 128
PIECE = 16
LEVELS = 4
INWARD, MIDDLE, OUTWARD, ACROSS, SHARE, REST, KEPT, CORE, WHOLE, KINDS = range(10)
WAYS = ("x", "x", "x", "z", "x", "x", "x", "w")
ORDER = (
    ("B", "hs", 0), ("B", "p", 0), ("B", "p", 1), ("B", "p", 4), ("E", "1", 0), ("M", "1", 0),
    ("B", "p", 5), ("E", "1", 1), ("E", "1", 2), ("E", "1", 3), ("M", "1", 1), ("M", "1", 2),
    ("B", "mask", 0), ("E", "1", 4), ("M", "1", 4), ("B", "loc", 0), ("B", "hs", 1),
    ("E", "2", 0), ("E", "1", 5), ("E", "1", 6), ("M", "1", 5), ("M", "2", 0), ("M", "1", 6),
    ("B", "ht", 0), ("B", "loc", 1), ("E", "2", 1), ("M", "2", 1), ("B", "loc", 2), ("E", "2", 2),
    ("E", "1", 7), ("M", "2", 2), ("M", "2", 3), ("M", "1", 7), ("B", "loc", 3), ("E", "2", 4),
    ("M", "2", 4), ("M", "3", 0), ("M", "3", 3), ("M", "3", 1), ("B", "ht", 1), ("B", "hs", 2),
    ("E", "2", 5), ("E", "2", 6), ("M", "2", 5), ("M", "3", 2), ("M", "2", 6), ("M", "4", 0),
    ("M", "4", 3), ("B", "hs", 3), ("E", "2", 7), ("E", "5", 0), ("M", "4", 1), ("M", "2", 7),
    ("M", "3", 4), ("M", "4", 2), ("M", "5", 3), ("M", "3", 5), ("B", "ht", 2), ("E", "5", 1),
    ("E", "5", 2), ("E", "3", 7), ("M", "5", 0), ("M", "7", 3), ("M", "3", 6), ("M", "7", 0),
    ("M", "4", 4), ("M", "4", 5), ("B", "ht", 3), ("E", "6", 3), ("E", "6", 0), ("E", "7", 3),
    ("E", "5", 4), ("E", "7", 0), ("E", "6", 1), ("E", "5", 5), ("E", "7", 1), ("M", "5", 1),
    ("M", "4", 6), ("M", "3", 7), ("M", "7", 1), ("B", "app", 0), ("E", "6", 2), ("E", "5", 6),
    ("E", "6", 4), ("E", "7", 2), ("M", "5", 2), ("M", "5", 4), ("M", "7", 2), ("B", "app", 1),
    ("E", "7", 4), ("E", "6", 5), ("E", "4", 7), ("M", "7", 4), ("M", "5", 5), ("M", "5", 6),
    ("M", "7", 5), ("M", "7", 6), ("M", "4", 7), ("B", "cmb", 0), ("E", "6", 6), ("E", "7", 5),
    ("M", "7", 7), ("B", "app", 2), ("E", "7", 6), ("E", "7", 7), ("B", "app", 3),
    ("B", "cmb", 1), ("B", "fin", 0), ("B", "cmb", 2), ("B", "cmb", 3), ("B", "fin", 1),
    ("B", "fin", 2), ("B", "fin", 3),
)


CONTRACT_CELLS = (((1,), (1,)), ((), ()))


def padded_2(cells, sides, width):
    for axis, dim in sides:
        count = lax.axis_size(axis)
        head = lax.slice_in_dim(cells, 0, width, axis=dim)
        tail = lax.slice_in_dim(cells, cells.shape[dim] - width, cells.shape[dim], axis=dim)
        cells = jnp.concatenate(
            [
                lax.ppermute(tail, axis, [(i, (i + 1) % count) for i in range(count)]),
                cells,
                lax.ppermute(head, axis, [((i + 1) % count, i) for i in range(count)]),
            ],
            axis=dim,
        )
    return cells


def slab_laplacian(padded, depth):
    centre = padded[:, 6 : 6 + depth]
    result = 3.0 * COEFFS[0] * centre
    for offset in range(1, 7):
        result = result + COEFFS[offset] * (
            padded[:, 6 + offset : 6 + offset + depth] + padded[:, 6 - offset : 6 - offset + depth]
        )
    for axis_number in (2, 3):
        for offset in range(1, 7):
            result = result + COEFFS[offset] * (
                jnp.roll(centre, offset, axis_number) + jnp.roll(centre, -offset, axis_number)
            )
    return result


def plain_shards(
    response, orbitals, projectors, potential, perturbing, energies, window_start, block_count
):
    band_rows = response.shape[0]
    local_cells = response.shape[1]
    devices = lax.axis_size("band")
    cells = local_cells * devices
    plane = GY * GZ
    depth = local_cells // plane
    ace_scale = 1.0 / math.sqrt(cells * projectors.shape[0])
    window_scale = 1.0 / math.sqrt(cells * band_rows)
    padded = padded_2(response.reshape(band_rows, depth, plane), (("band", 1),), 6)
    padded_wide = padded.astype(jnp.float32).reshape(band_rows, depth + 12, GY, GZ)
    kinetic = -KINETIC * slab_laplacian(padded_wide, depth).reshape(band_rows, local_cells)
    response_wide = response.astype(jnp.float32)
    picked = response
    share = lax.psum_scatter(
        lax.dot_general(picked, projectors, CONTRACT_CELLS, preferred_element_type=jnp.float32),
        "band",
        scatter_dimension=0,
        tiled=True,
    )
    ace_intersection = lax.all_gather(
        (share * ace_scale).astype(jnp.bfloat16), "band", axis=0, tiled=True
    )
    ace_term = -jnp.dot(ace_intersection, projectors, preferred_element_type=jnp.float32)
    applied = (
        kinetic + potential[None, :] * response_wide + ace_term - energies[:, None] * response_wide
    )
    orbitals_wide = orbitals.astype(jnp.float32)
    unprojected = -(perturbing[None, :] * orbitals_wide) - applied
    unprojected_low = unprojected.astype(jnp.bfloat16)
    picked = unprojected_low
    window_share = lax.psum_scatter(
        lax.dot_general(picked, orbitals, CONTRACT_CELLS, preferred_element_type=jnp.float32),
        "band",
        scatter_dimension=0,
        tiled=True,
    )
    window_intersection = lax.all_gather(
        (window_share * window_scale).astype(jnp.bfloat16), "band", axis=0, tiled=True
    )
    block_ids = jnp.arange(band_rows, dtype=jnp.int32) // (band_rows // NBLK)
    lowest = window_start[:, None]
    highest = window_start[:, None] + block_count[:, None] - 1
    inside = (block_ids[None, :] >= lowest) & (block_ids[None, :] <= highest)
    window_intersection = jnp.where(
        inside, window_intersection, jnp.zeros_like(window_intersection)
    )
    residual_wide = unprojected - jnp.dot(
        window_intersection, orbitals, preferred_element_type=jnp.float32
    )
    updated_response = (response_wide + STEP_SIZE * residual_wide).astype(jnp.bfloat16)
    return (updated_response, residual_wide.astype(jnp.bfloat16))


def plane_operator():
    plane = GY * GZ
    op = np.zeros((plane, plane), np.float64)
    for y in range(GY):
        for z in range(GZ):
            out = y * GZ + z
            op[out, out] += 3.0 * COEFFS[0]
            for k in range(1, HALO + 1):
                for sign in (-k, k):
                    op[((y + sign) % GY) * GZ + z, out] += COEFFS[k]
                    op[y * GZ + (z + sign) % GZ, out] += COEFFS[k]
    return (KINETIC * op).astype(np.float32)


def kernel(
    count, ace_scale, window_scale,
    resp_hbm, orb_hbm, proj_hbm, pot, pert, energies, first, blocks, op_hi, op_lo,
    updated_hbm, residual_hbm,
    resp, orb, proj, halo_l, halo_r, unp, acc, c_send, c_recv, e_send, e_recv, z_send, z_recv,
    x_send, x_recv, full, w_sum, w_send, w_recv, w_full, inside, energy, updated, residual,
    send_sem, recv_sem, halo_send, halo_recv, load_sem, ws_send, ws_recv, wg_send, wg_recv, out_sem,
):
    rows, cells = resp.shape
    plane = GY * GZ
    depth = cells // plane
    height = rows // GROUPS
    half, quarter = height // 2, height // 4
    pieces = proj.shape[0] // CHUNK
    total = GROUPS * pieces
    block = rows // NBLK
    reach = REACH * block

    me = lax.axis_index("band")
    core = me % 2
    across = (me // 2) % 2
    level = me // 4
    edge = (level == 0) | (level == LEVELS - 1)
    mid = jnp.logical_not(edge)
    upper = level // 2
    left, right = (me + count - 1) % count, (me + 1) % count
    core_peer = me + 1 - 2 * core
    x_peer = me + 2 - 4 * across
    e_peer = me + 4 - 8 * (level % 2)
    m_peer = (LEVELS - 1 - level) * 4 + me % 4
    everyone = [(me + k) % count for k in range(1, count)]

    def remote(src, dst, send, recv, device):
        return pltpu.make_async_remote_copy(
            src_ref=src, dst_ref=dst, send_sem=send, recv_sem=recv,
            device_id={"band": device}, device_id_type=pl.DeviceIdType.MESH,
        )

    loads = [pltpu.make_async_copy(resp_hbm, resp, load_sem.at[0])]
    for j in range(pieces):
        at = pl.ds(j * CHUNK, CHUNK)
        loads.append(
            pltpu.make_async_copy(proj_hbm.at[at, :], proj.at[at, :], load_sem.at[1 + j])
        )
    loads.append(pltpu.make_async_copy(orb_hbm, orb, load_sem.at[1 + pieces]))
    for load in loads:
        load.start()

    barrier = pltpu.get_barrier_semaphore()
    for device in everyone:
        pl.semaphore_signal(
            barrier, inc=1, device_id={"band": device}, device_id_type=pl.DeviceIdType.MESH
        )

    core_row = pl.multiple_of(core * half, half)
    other_row = pl.multiple_of((1 - core) * half, half)

    def span(g):
        return slice(g * height, (g + 1) * height)

    halos = []
    for g in range(GROUPS):
        at = pl.ds(g * height, height)
        halos.append((
            remote(
                resp.at[at, :], halo_l.at[at, :], halo_send.at[g, 0], halo_recv.at[g, 0], right
            ),
            remote(
                resp.at[at, :], halo_r.at[at, :], halo_send.at[g, 1], halo_recv.at[g, 1], left
            ),
        ))

    def halo_start(g):
        for copy in halos[g]:
            copy.start()

    def rest_rows(offset, size):
        return pl.ds(pl.multiple_of(core_row + offset, PIECE), size)

    sixteenth = half // LEVELS
    z_ring = [(level + k) % LEVELS for k in range(1, LEVELS)]

    def copy_of(q, kind):
        sems = (send_sem.at[q, kind], recv_sem.at[q, kind])
        way = WAYS[q]
        if kind == CORE:
            return remote(c_send.at[q], c_recv.at[q], *sems, core_peer)
        if kind == WHOLE:
            whole = full.at[q, pl.ds(core_row, half), :]
            return remote(whole, whole, *sems, core_peer)
        if way == "w":
            if kind == ACROSS:
                at = pl.ds(0, sixteenth)
                return remote(x_send.at[q, at, :], x_recv.at[q, at, :], *sems, x_peer)
            k = kind % 4
            device = z_ring[k] * 4 + me % 4
            if kind < SHARE:
                there = pl.ds(pl.multiple_of(z_ring[k] * sixteenth, sixteenth), sixteenth)
                here = pl.ds(k * sixteenth, sixteenth)
                return remote(e_send.at[q, there, :], e_recv.at[q, here, :], *sems, device)
            mine = full.at[q, rest_rows(level * sixteenth, sixteenth), :]
            return remote(mine, mine, *sems, device)
        along = way == "z"
        own = (upper if along else across) * quarter
        if kind == INWARD:
            if along:
                return remote(e_send.at[q], e_recv.at[q], *sems, e_peer)
            small = pl.ds(0, quarter)
            return remote(e_send.at[q, small, :], e_recv.at[q, small, :], *sems, e_peer)
        if kind == MIDDLE:
            return remote(z_send.at[q], z_recv.at[q], *sems, m_peer)
        if kind == ACROSS:
            return remote(x_send.at[q], x_recv.at[q], *sems, x_peer)
        mine = full.at[q, rest_rows(own, quarter), :]
        if kind == SHARE:
            return remote(mine, mine, *sems, m_peer if along else x_peer)
        if kind == OUTWARD:
            return remote(mine, mine, *sems, e_peer)
        rest = full.at[q, rest_rows((1 - upper) * quarter, quarter), :]
        return remote(rest, rest, *sems, e_peer)

    sent = {}

    def start(role, q, *kinds):
        for kind in kinds:
            copy_of(q, kind).start()
            sent.setdefault(role, []).append((q, kind))

    def wait(q, *kinds):
        for kind in kinds:
            copy_of(q, kind).wait_recv()

    low, wider = jnp.bfloat16, jnp.float32

    def partials(pair, h):
        if pair == 0:
            loads[1 + h].wait()
        value = lax.dot_general(
            resp[pair * 2 * height : (pair + 1) * 2 * height, :],
            proj[h * CHUNK : (h + 1) * CHUNK, :], NT, preferred_element_type=wider,
        )
        for k in range(2):
            q = (2 * pair + k) * pieces + h
            acc[q] = value[k * height : (k + 1) * height]
            c_send[q] = acc[q, pl.ds(other_row, half), :].astype(low)
            start("B", q, CORE)

    def core_sum(q, offset, size):
        if not isinstance(offset, int):
            offset = pl.multiple_of(offset, PIECE)
        at = pl.multiple_of(core_row + offset, PIECE)
        return acc[q, pl.ds(at, size), :] + c_recv[q, pl.ds(offset, size), :].astype(wider)

    def held(q, offset):
        return acc.at[q, rest_rows(offset, quarter), :]

    def along_z(role, s, q):
        mine, rest = upper * quarter, (1 - upper) * quarter
        if s == 1:
            wait(q, CORE)
            e_send[q] = core_sum(q, 0, half).astype(low)
            start(role, q, INWARD)
        if s == 2:
            wait(q, CORE, INWARD)
            at = pl.ds(pl.multiple_of(rest, quarter), quarter)
            z_send[q] = (core_sum(q, rest, quarter) + e_recv[q, at, :].astype(wider)).astype(low)
            start(role, q, MIDDLE)
            at = pl.ds(pl.multiple_of(mine, quarter), quarter)
            held(q, mine)[...] = core_sum(q, mine, quarter) + e_recv[q, at, :].astype(wider)
        if s == 3:
            wait(q, MIDDLE)
            value = held(q, mine)[...] + z_recv[q].astype(wider)
            x_send[q] = value.astype(low)
            start(role, q, ACROSS)
            held(q, mine)[...] = value
        if s == 4:
            wait(q, ACROSS)
            value = held(q, mine)[...] + x_recv[q].astype(wider)
            full[q, rest_rows(mine, quarter), :] = (value * ace_scale).astype(low)
            start(role, q, SHARE, OUTWARD)
        if s == 5:
            wait(q, SHARE)
            start(role, q, REST, WHOLE)
        if s == 6:
            wait(q, OUTWARD, REST)
            start(role, q, WHOLE)

    def along_x(role, s, q):
        mine, rest = across * quarter, (1 - across) * quarter
        if s == 1:
            wait(q, CORE)
            x_send[q] = core_sum(q, rest, quarter).astype(low)
            start(role, q, ACROSS)
        if s == 2:
            wait(q, ACROSS)
            value = core_sum(q, mine, quarter) + x_recv[q].astype(wider)
            if role == "E":
                e_send[q, :quarter, :] = value.astype(low)
                start(role, q, INWARD)
            else:
                held(q, mine)[...] = value
        if s == 3:
            wait(q, INWARD)
            value = held(q, mine)[...] + e_recv[q, :quarter, :].astype(wider)
            z_send[q] = value.astype(low)
            start(role, q, MIDDLE)
            held(q, mine)[...] = value
        if s == 4:
            wait(q, MIDDLE)
            value = held(q, mine)[...] + z_recv[q].astype(wider)
            full[q, rest_rows(mine, quarter), :] = (value * ace_scale).astype(low)
            start(role, q, OUTWARD, SHARE)
        if s == 5 and role == "E":
            wait(q, OUTWARD)
            start(role, q, SHARE)
        if s == 5 and role == "M":
            wait(q, SHARE)
            start(role, q, WHOLE)
        if s == 6:
            wait(q, SHARE)
            start(role, q, WHOLE)

    def direct(role, s, q):
        if s == 1:
            wait(q, CORE)
            e_send[q] = core_sum(q, 0, half).astype(low)
            start(role, q, 0, 1, 2)
        if s == 2:
            wait(q, 0, 1, 2)
            value = core_sum(q, level * sixteenth, sixteenth)
            for k in range(LEVELS - 1):
                at = slice(k * sixteenth, (k + 1) * sixteenth)
                value = value + e_recv[q, at, :].astype(wider)
            x_send[q, :sixteenth, :] = value.astype(low)
            start(role, q, ACROSS)
            acc[q, rest_rows(level * sixteenth, sixteenth), :] = value
        if s == 3:
            wait(q, ACROSS)
            at = rest_rows(level * sixteenth, sixteenth)
            value = acc[q, at, :] + x_recv[q, :sixteenth, :].astype(wider)
            full[q, at, :] = (value * ace_scale).astype(low)
            start(role, q, 4, 5, 6)
        if s == 4:
            wait(q, 4, 5, 6)
            start(role, q, WHOLE)

    chains = {"z": along_z, "x": along_x, "w": direct}

    def column(ref):
        return jnp.broadcast_to(ref[...].astype(wider), (plane, rows)).T

    def window(g):
        return min(max(g * height - reach, 0), rows - WINDOW)

    def masks():
        begin = column(first)
        end = begin + column(blocks)
        lanes = lax.broadcasted_iota(jnp.int32, (height, TILE), 1).astype(wider)
        for g in range(GROUPS):
            for t in range(WINDOW // TILE):
                ids = jnp.floor((lanes + float(window(g) + t * TILE)) * (1.0 / block))
                keep = (ids >= begin[span(g)]) & (ids < end[span(g)])
                inside[g, t] = jnp.where(keep, 1.0, 0.0)
        energy[...] = column(energies)

    def local_terms(g):
        for p in range(depth):
            cut = resp[span(g), p * plane : (p + 1) * plane]
            unp[span(g), p * plane : (p + 1) * plane] = jnp.dot(
                cut, op_hi[...], preferred_element_type=wider
            ) + jnp.dot(cut, op_lo[...], preferred_element_type=wider)

        @pl.loop(0, height // ROWS)
        def _(i):
            at = pl.ds(pl.multiple_of(g * height + i * ROWS, ROWS), ROWS)
            planes = [resp[at, p * plane : (p + 1) * plane].astype(wider) for p in range(depth)]
            level_of = energy[at, :]
            for p in range(depth):
                cut = slice(p * plane, (p + 1) * plane)
                value = unp[at, cut] + (level_of - pot[cut]) * planes[p]
                value = value - pert[cut] * orb[at, cut].astype(wider)
                for k in range(1, HALO + 1):
                    for q in (p - k, p + k):
                        if 0 <= q < depth:
                            value = value + (KINETIC * COEFFS[k]) * planes[q]
                unp[at, cut] = value

    def halo_terms(g):
        for copy in halos[g]:
            copy.wait_recv()

        @pl.loop(0, height // ROWS)
        def _(i):
            at = pl.ds(pl.multiple_of(g * height + i * ROWS, ROWS), ROWS)
            before = [
                halo_l[at, p * plane : (p + 1) * plane].astype(wider) for p in range(HALO)
            ]
            after = [
                halo_r[at, p * plane : (p + 1) * plane].astype(wider) for p in range(HALO)
            ]
            for p in range(depth):
                value = unp[at, p * plane : (p + 1) * plane]
                for k in range(1, HALO + 1):
                    if p - k < 0:
                        value = value + (KINETIC * COEFFS[k]) * before[HALO + p - k]
                    if p + k >= depth:
                        value = value + (KINETIC * COEFFS[k]) * after[p + k - depth]
                unp[at, p * plane : (p + 1) * plane] = value

    def place(device):
        return pl.ds(pl.multiple_of((device // 2) * PIECE, PIECE), PIECE), device % 2

    def apply(g):
        weights = jnp.concatenate([full[g * pieces + h] for h in range(pieces)], axis=1)
        low_parts = []
        for lo in range(0, cells, WINDOW):
            value = unp[span(g), lo : lo + WINDOW] + jnp.dot(
                weights, proj[:, lo : lo + WINDOW], preferred_element_type=wider
            )
            unp[span(g), lo : lo + WINDOW] = value
            low_parts.append(value.astype(low))
        value = lax.dot_general(
            jnp.concatenate(low_parts, axis=1), orb[window(g) : window(g) + WINDOW, :], NT,
            preferred_element_type=wider,
        )
        for t in range(WINDOW // TILE):
            w_sum[g, t] = value[:, t * TILE : (t + 1) * TILE]
            w_send[g, t] = value[:, t * TILE : (t + 1) * TILE].astype(low)
        for k, device in enumerate(everyone):
            at, t = place(device)
            remote(
                w_send.at[g, t, at, :], w_recv.at[g, k], ws_send.at[g], ws_recv.at[g], device
            ).start()

    def drain(sem, g):
        pltpu.make_async_copy(w_recv.at[g], w_recv.at[g], sem.at[g]).wait()

    def combine(g):
        drain(ws_recv, g)
        at, t = place(me)
        value = w_sum[g, t, at, :]
        for k in range(count - 1):
            value = value + w_recv[g, k].astype(wider)
        w_full[g, t, at, :] = (value * window_scale).astype(low)
        mine = w_full.at[g, t, at, :]
        for device in everyone:
            remote(mine, mine, wg_send.at[g], wg_recv.at[g], device).start()

    outs = []
    for g in range(GROUPS):
        for i, (src, dst) in enumerate(((updated, updated_hbm), (residual, residual_hbm))):
            outs.append(
                pltpu.make_async_copy(src.at[span(g), :], dst.at[span(g), :], out_sem.at[g, i])
            )

    def finish(g):
        drain(wg_recv, g)
        weights = jnp.concatenate(
            [
                (w_full[g, t].astype(wider) * inside[g, t]).astype(low)
                for t in range(WINDOW // TILE)
            ],
            axis=1,
        )
        for lo in range(0, cells, WINDOW):
            at = (span(g), slice(lo, lo + WINDOW))
            value = unp[at] - jnp.dot(
                weights, orb[window(g) : window(g) + WINDOW, lo : lo + WINDOW],
                preferred_element_type=wider,
            )
            residual[at] = value.astype(low)
            updated[at] = (resp[at].astype(wider) + STEP_SIZE * value).astype(low)
        outs[2 * g].start()
        outs[2 * g + 1].start()

    def orbitals_ready():
        loads[1 + pieces].wait()
        masks()

    common = {
        "hs": halo_start, "loc": local_terms, "ht": halo_terms,
        "app": apply, "cmb": combine, "fin": finish,
    }

    def perform(role, name, number):
        if name == "p":
            partials(number // (2 * pieces), number % (2 * pieces))
        elif name == "mask":
            orbitals_ready()
        elif name in common:
            common[name](number)
        elif name == "7":
            wait(number, WHOLE)
        else:
            chains[WAYS[number]](role, int(name), number)

    loads[0].wait()
    pl.semaphore_wait(barrier, count - 1)
    for role, run in itertools.groupby(ORDER, key=lambda step: step[0]):
        run = list(run)

        def body():
            for step in run:
                perform(*step)

        if role == "B":
            body()
        else:
            pl.when(edge if role == "E" else mid)(body)

    for copy in outs:
        copy.wait()
    for g in range(GROUPS):
        for copy in halos[g]:
            copy.wait_send()
        drain(ws_send, g)
        drain(wg_send, g)
    for role, condition in (("B", None), ("E", edge), ("M", mid)):
        def body():
            for q, kind in sent[role]:
                copy_of(q, kind).wait_send()

        if condition is None:
            body()
        else:
            pl.when(condition)(body)


def hand_over(updated, residual, updated_out, residual_out, first, second, in_sem, out_sem):
    height = first.shape[0] // GROUPS
    copies = []
    for g in range(GROUPS):
        at = pl.ds(g * height, height)
        for i, (src, held, dst) in enumerate(
            ((updated, first, updated_out), (residual, second, residual_out))
        ):
            copies.append((
                pltpu.make_async_copy(src.at[at, :], held.at[at, :], in_sem.at[g, i]),
                pltpu.make_async_copy(held.at[at, :], dst.at[at, :], out_sem.at[g, i]),
            ))
    for come, _ in copies:
        come.start()
    for come, go in copies:
        come.wait()
        go.start()
    for _, go in copies:
        go.wait()


def shards(
    response, orbitals, projectors, potential, perturbing, energies, window_start, block_count
):
    rows, local = response.shape
    count = lax.axis_size("band")
    cells = local * count
    pieces = projectors.shape[0] // CHUNK
    total = GROUPS * pieces
    height = rows // GROUPS
    half, quarter = height // 2, height // 4
    op = plane_operator()
    op_hi = jnp.asarray(op).astype(jnp.bfloat16)
    op_lo = (jnp.asarray(op) - op_hi.astype(jnp.float32)).astype(jnp.bfloat16)
    low, wider = jnp.bfloat16, jnp.float32
    tiles = WINDOW // TILE
    vmem = pl.BlockSpec(memory_space=pltpu.VMEM)
    hbm = pl.BlockSpec(memory_space=pl.ANY)
    made = pl.pallas_call(
        functools.partial(
            kernel, count,
            1.0 / math.sqrt(cells * projectors.shape[0]), 1.0 / math.sqrt(cells * rows),
        ),
        out_shape=(jax.ShapeDtypeStruct(response.shape, low),) * 2,
        in_specs=[hbm] * 3 + [vmem] * 7,
        out_specs=(hbm, hbm),
        scratch_shapes=[
            pltpu.VMEM(response.shape, low),
            pltpu.VMEM(orbitals.shape, low),
            pltpu.VMEM(projectors.shape, low),
            pltpu.VMEM(response.shape, low),
            pltpu.VMEM(response.shape, low),
            pltpu.VMEM(response.shape, wider),
            pltpu.VMEM((total, height, CHUNK), wider),
            pltpu.VMEM((total, half, CHUNK), low),
            pltpu.VMEM((total, half, CHUNK), low),
            pltpu.VMEM((total, half, CHUNK), low),
            pltpu.VMEM((total, half, CHUNK), low),
            pltpu.VMEM((total, quarter, CHUNK), low),
            pltpu.VMEM((total, quarter, CHUNK), low),
            pltpu.VMEM((total, quarter, CHUNK), low),
            pltpu.VMEM((total, quarter, CHUNK), low),
            pltpu.VMEM((total, height, CHUNK), low),
            pltpu.VMEM((GROUPS, tiles, height, TILE), wider),
            pltpu.VMEM((GROUPS, tiles, height, TILE), low),
            pltpu.VMEM((GROUPS, count - 1, PIECE, TILE), low),
            pltpu.VMEM((GROUPS, tiles, height, TILE), low),
            pltpu.VMEM((GROUPS, tiles, height, TILE), wider),
            pltpu.VMEM((rows, GY * GZ), wider),
            pltpu.VMEM(response.shape, low),
            pltpu.VMEM(response.shape, low),
            pltpu.SemaphoreType.DMA((total, KINDS)),
            pltpu.SemaphoreType.DMA((total, KINDS)),
            pltpu.SemaphoreType.DMA((GROUPS, 2)),
            pltpu.SemaphoreType.DMA((GROUPS, 2)),
            pltpu.SemaphoreType.DMA((pieces + 2,)),
            pltpu.SemaphoreType.DMA((GROUPS,)),
            pltpu.SemaphoreType.DMA((GROUPS,)),
            pltpu.SemaphoreType.DMA((GROUPS,)),
            pltpu.SemaphoreType.DMA((GROUPS,)),
            pltpu.SemaphoreType.DMA((GROUPS, 2)),
        ],
        compiler_params=pltpu.CompilerParams(
            collective_id=0, has_side_effects=True, vmem_limit_bytes=56 * 1024 * 1024
        ),
    )(
        response, orbitals, projectors,
        potential, perturbing,
        energies[None, :], window_start[None, :], block_count[None, :],
        op_hi, op_lo,
    )
    return pl.pallas_call(
        hand_over,
        out_shape=(jax.ShapeDtypeStruct(response.shape, low),) * 2,
        in_specs=[hbm, hbm],
        out_specs=(hbm, hbm),
        scratch_shapes=[pltpu.VMEM(response.shape, low)] * 2
        + [pltpu.SemaphoreType.DMA((GROUPS, 2))] * 2,
        compiler_params=pltpu.CompilerParams(vmem_limit_bytes=60 * 1024 * 1024),
    )(*made)


def solution(mesh):
    fits = mesh.shape["band"] == 4 * LEVELS
    in_specs = (
        P("pert", "band"),
        P(None, "band"),
        P(None, "band"),
        P("band"),
        P(("pert", "band")),
        P(),
        P(),
        P(),
    )
    out_specs = (P("pert", "band"), P("pert", "band"))
    return jax.shard_map(
        shards if fits else plain_shards,
        mesh=mesh, in_specs=in_specs, out_specs=out_specs, check_vma=False,
    )
```

```python
import functools
import itertools
import math

import jax
import jax.numpy as jnp
import numpy as np
from jax import lax
from jax.experimental import pallas as pl
from jax.experimental.pallas import tpu as pltpu
from jax.sharding import PartitionSpec as P

GY = 8
GZ = 16
NBLK = 32
REACH = 4


COEFFS = (
    -5369.0 / 1800.0,
    12.0 / 7.0,
    -15.0 / 56.0,
    10.0 / 189.0,
    -1.0 / 112.0,
    2.0 / 1925.0,
    -1.0 / 16632.0,
)
KINETIC = 0.125
STEP_SIZE = 0.3
HALO = 6
NT = (((1,), (1,)), ((), ()))
GROUPS = 4
CHUNK = 1024
WINDOW = 256
ROWS = 32
TILE = 128
PIECE = 16
LEVELS = 4
INWARD, MIDDLE, OUTWARD, ACROSS, SHARE, REST, KEPT, CORE, WHOLE, KINDS = range(10)
WAYS = ("x", "x", "x", "z", "x", "x", "x", "w")
ORDER = (
    ("B", "hs", 0), ("B", "p", 0), ("B", "p", 1), ("B", "p", 4), ("E", "1", 0), ("M", "1", 0),
    ("B", "p", 5), ("E", "1", 1), ("E", "1", 2), ("E", "1", 3), ("M", "1", 1), ("M", "1", 2),
    ("B", "mask", 0), ("E", "1", 4), ("M", "1", 4), ("B", "loc", 0), ("B", "hs", 1),
    ("E", "2", 0), ("E", "1", 5), ("E", "1", 6), ("M", "1", 5), ("M", "2", 0), ("M", "1", 6),
    ("B", "ht", 0), ("B", "loc", 1), ("E", "2", 1), ("M", "2", 1), ("B", "loc", 2), ("E", "2", 2),
    ("E", "1", 7), ("M", "2", 2), ("M", "2", 3), ("M", "1", 7), ("B", "loc", 3), ("E", "2", 4),
    ("M", "2", 4), ("M", "3", 0), ("M", "3", 3), ("M", "3", 1), ("B", "ht", 1), ("B", "hs", 2),
    ("E", "2", 5), ("E", "2", 6), ("M", "2", 5), ("M", "3", 2), ("M", "2", 6), ("M", "4", 0),
    ("M", "4", 3), ("B", "hs", 3), ("E", "2", 7), ("E", "5", 0), ("M", "4", 1), ("M", "2", 7),
    ("M", "3", 4), ("M", "4", 2), ("M", "5", 3), ("M", "3", 5), ("E", "5", 1), ("E", "5", 2),
    ("E", "3", 7), ("M", "5", 0), ("M", "7", 3), ("M", "3", 6), ("M", "7", 0), ("M", "4", 4),
    ("M", "4", 5), ("E", "6", 3), ("E", "6", 0), ("E", "7", 3), ("E", "5", 4), ("E", "7", 0),
    ("E", "6", 1), ("E", "5", 5), ("E", "7", 1), ("M", "5", 1), ("M", "4", 6), ("M", "3", 7),
    ("M", "7", 1), ("B", "app", 0), ("E", "6", 2), ("E", "5", 6), ("E", "6", 4), ("E", "7", 2),
    ("M", "5", 2), ("M", "5", 4), ("M", "7", 2), ("B", "app", 1), ("E", "7", 4), ("E", "6", 5),
    ("E", "4", 7), ("M", "7", 4), ("M", "5", 5), ("M", "5", 6), ("M", "7", 5), ("M", "7", 6),
    ("M", "4", 7), ("B", "cmb", 0), ("E", "6", 6), ("E", "7", 5), ("M", "7", 7), ("B", "ht", 2),
    ("B", "app", 2), ("E", "7", 6), ("E", "7", 7), ("B", "ht", 3), ("B", "app", 3),
    ("B", "cmb", 1), ("B", "fin", 0), ("B", "cmb", 2), ("B", "cmb", 3), ("B", "fin", 1),
    ("B", "fin", 2), ("B", "fin", 3),
)


CONTRACT_CELLS = (((1,), (1,)), ((), ()))


def padded_2(cells, sides, width):
    for axis, dim in sides:
        count = lax.axis_size(axis)
        head = lax.slice_in_dim(cells, 0, width, axis=dim)
        tail = lax.slice_in_dim(cells, cells.shape[dim] - width, cells.shape[dim], axis=dim)
        cells = jnp.concatenate(
            [
                lax.ppermute(tail, axis, [(i, (i + 1) % count) for i in range(count)]),
                cells,
                lax.ppermute(head, axis, [((i + 1) % count, i) for i in range(count)]),
            ],
            axis=dim,
        )
    return cells


def slab_laplacian(padded, depth):
    centre = padded[:, 6 : 6 + depth]
    result = 3.0 * COEFFS[0] * centre
    for offset in range(1, 7):
        result = result + COEFFS[offset] * (
            padded[:, 6 + offset : 6 + offset + depth] + padded[:, 6 - offset : 6 - offset + depth]
        )
    for axis_number in (2, 3):
        for offset in range(1, 7):
            result = result + COEFFS[offset] * (
                jnp.roll(centre, offset, axis_number) + jnp.roll(centre, -offset, axis_number)
            )
    return result


def plain_shards(
    response, orbitals, projectors, potential, perturbing, energies, window_start, block_count
):
    band_rows = response.shape[0]
    local_cells = response.shape[1]
    devices = lax.axis_size("band")
    cells = local_cells * devices
    plane = GY * GZ
    depth = local_cells // plane
    ace_scale = 1.0 / math.sqrt(cells * projectors.shape[0])
    window_scale = 1.0 / math.sqrt(cells * band_rows)
    padded = padded_2(response.reshape(band_rows, depth, plane), (("band", 1),), 6)
    padded_wide = padded.astype(jnp.float32).reshape(band_rows, depth + 12, GY, GZ)
    kinetic = -KINETIC * slab_laplacian(padded_wide, depth).reshape(band_rows, local_cells)
    response_wide = response.astype(jnp.float32)
    picked = response
    share = lax.psum_scatter(
        lax.dot_general(picked, projectors, CONTRACT_CELLS, preferred_element_type=jnp.float32),
        "band",
        scatter_dimension=0,
        tiled=True,
    )
    ace_intersection = lax.all_gather(
        (share * ace_scale).astype(jnp.bfloat16), "band", axis=0, tiled=True
    )
    ace_term = -jnp.dot(ace_intersection, projectors, preferred_element_type=jnp.float32)
    applied = (
        kinetic + potential[None, :] * response_wide + ace_term - energies[:, None] * response_wide
    )
    orbitals_wide = orbitals.astype(jnp.float32)
    unprojected = -(perturbing[None, :] * orbitals_wide) - applied
    unprojected_low = unprojected.astype(jnp.bfloat16)
    picked = unprojected_low
    window_share = lax.psum_scatter(
        lax.dot_general(picked, orbitals, CONTRACT_CELLS, preferred_element_type=jnp.float32),
        "band",
        scatter_dimension=0,
        tiled=True,
    )
    window_intersection = lax.all_gather(
        (window_share * window_scale).astype(jnp.bfloat16), "band", axis=0, tiled=True
    )
    block_ids = jnp.arange(band_rows, dtype=jnp.int32) // (band_rows // NBLK)
    lowest = window_start[:, None]
    highest = window_start[:, None] + block_count[:, None] - 1
    inside = (block_ids[None, :] >= lowest) & (block_ids[None, :] <= highest)
    window_intersection = jnp.where(
        inside, window_intersection, jnp.zeros_like(window_intersection)
    )
    residual_wide = unprojected - jnp.dot(
        window_intersection, orbitals, preferred_element_type=jnp.float32
    )
    updated_response = (response_wide + STEP_SIZE * residual_wide).astype(jnp.bfloat16)
    return (updated_response, residual_wide.astype(jnp.bfloat16))


def plane_operator():
    plane = GY * GZ
    op = np.zeros((plane, plane), np.float64)
    for y in range(GY):
        for z in range(GZ):
            out = y * GZ + z
            op[out, out] += 3.0 * COEFFS[0]
            for k in range(1, HALO + 1):
                for sign in (-k, k):
                    op[((y + sign) % GY) * GZ + z, out] += COEFFS[k]
                    op[y * GZ + (z + sign) % GZ, out] += COEFFS[k]
    return (KINETIC * op).astype(np.float32)


def kernel(
    count, ace_scale, window_scale,
    resp_hbm, orb_hbm, proj_hbm, pot, pert, energies, first, blocks, op_hi, op_lo,
    updated_hbm, residual_hbm,
    resp, orb, proj, halo_l, halo_r, unp, acc, c_send, c_recv, e_send, e_recv, z_send, z_recv,
    x_send, x_recv, full, w_sum, w_send, w_recv, w_full, inside, energy, updated, residual,
    send_sem, recv_sem, halo_send, halo_recv, load_sem, ws_send, ws_recv, wg_send, wg_recv, out_sem,
):
    rows, cells = resp.shape
    plane = GY * GZ
    depth = cells // plane
    height = rows // GROUPS
    half, quarter = height // 2, height // 4
    pieces = proj.shape[0] // CHUNK
    total = GROUPS * pieces
    block = rows // NBLK
    reach = REACH * block

    me = lax.axis_index("band")
    core = me % 2
    across = (me // 2) % 2
    level = me // 4
    edge = (level == 0) | (level == LEVELS - 1)
    mid = jnp.logical_not(edge)
    upper = level // 2
    left, right = (me + count - 1) % count, (me + 1) % count
    core_peer = me + 1 - 2 * core
    x_peer = me + 2 - 4 * across
    e_peer = me + 4 - 8 * (level % 2)
    m_peer = (LEVELS - 1 - level) * 4 + me % 4
    everyone = [(me + k) % count for k in range(1, count)]

    def remote(src, dst, send, recv, device):
        return pltpu.make_async_remote_copy(
            src_ref=src, dst_ref=dst, send_sem=send, recv_sem=recv,
            device_id={"band": device}, device_id_type=pl.DeviceIdType.MESH,
        )

    loads = [pltpu.make_async_copy(resp_hbm, resp, load_sem.at[0])]
    for j in range(pieces):
        at = pl.ds(j * CHUNK, CHUNK)
        loads.append(
            pltpu.make_async_copy(proj_hbm.at[at, :], proj.at[at, :], load_sem.at[1 + j])
        )
    loads.append(pltpu.make_async_copy(orb_hbm, orb, load_sem.at[1 + pieces]))
    for load in loads:
        load.start()

    barrier = pltpu.get_barrier_semaphore()
    for device in everyone:
        pl.semaphore_signal(
            barrier, inc=1, device_id={"band": device}, device_id_type=pl.DeviceIdType.MESH
        )

    core_row = pl.multiple_of(core * half, half)
    other_row = pl.multiple_of((1 - core) * half, half)

    def span(g):
        return slice(g * height, (g + 1) * height)

    halos = []
    for g in range(GROUPS):
        at = pl.ds(g * height, height)
        halos.append((
            remote(
                resp.at[at, :], halo_l.at[at, :], halo_send.at[g, 0], halo_recv.at[g, 0], right
            ),
            remote(
                resp.at[at, :], halo_r.at[at, :], halo_send.at[g, 1], halo_recv.at[g, 1], left
            ),
        ))

    def halo_start(g):
        for copy in halos[g]:
            copy.start()

    def rest_rows(offset, size):
        return pl.ds(pl.multiple_of(core_row + offset, PIECE), size)

    sixteenth = half // LEVELS
    z_ring = [(level + k) % LEVELS for k in range(1, LEVELS)]

    def copy_of(q, kind):
        sems = (send_sem.at[q, kind], recv_sem.at[q, kind])
        way = WAYS[q]
        if kind == CORE:
            return remote(c_send.at[q], c_recv.at[q], *sems, core_peer)
        if kind == WHOLE:
            whole = full.at[q, pl.ds(core_row, half), :]
            return remote(whole, whole, *sems, core_peer)
        if way == "w":
            if kind == ACROSS:
                at = pl.ds(0, sixteenth)
                return remote(x_send.at[q, at, :], x_recv.at[q, at, :], *sems, x_peer)
            k = kind % 4
            device = z_ring[k] * 4 + me % 4
            if kind < SHARE:
                there = pl.ds(pl.multiple_of(z_ring[k] * sixteenth, sixteenth), sixteenth)
                here = pl.ds(k * sixteenth, sixteenth)
                return remote(e_send.at[q, there, :], e_recv.at[q, here, :], *sems, device)
            mine = full.at[q, rest_rows(level * sixteenth, sixteenth), :]
            return remote(mine, mine, *sems, device)
        along = way == "z"
        own = (upper if along else across) * quarter
        if kind == INWARD:
            if along:
                return remote(e_send.at[q], e_recv.at[q], *sems, e_peer)
            small = pl.ds(0, quarter)
            return remote(e_send.at[q, small, :], e_recv.at[q, small, :], *sems, e_peer)
        if kind == MIDDLE:
            return remote(z_send.at[q], z_recv.at[q], *sems, m_peer)
        if kind == ACROSS:
            return remote(x_send.at[q], x_recv.at[q], *sems, x_peer)
        mine = full.at[q, rest_rows(own, quarter), :]
        if kind == SHARE:
            return remote(mine, mine, *sems, m_peer if along else x_peer)
        if kind == OUTWARD:
            return remote(mine, mine, *sems, e_peer)
        rest = full.at[q, rest_rows((1 - upper) * quarter, quarter), :]
        return remote(rest, rest, *sems, e_peer)

    sent = {}

    def start(role, q, *kinds):
        for kind in kinds:
            copy_of(q, kind).start()
            sent.setdefault(role, []).append((q, kind))

    def wait(q, *kinds):
        for kind in kinds:
            copy_of(q, kind).wait_recv()

    low, wider = jnp.bfloat16, jnp.float32

    def partials(pair, h):
        if pair == 0:
            loads[1 + h].wait()
        value = lax.dot_general(
            resp[pair * 2 * height : (pair + 1) * 2 * height, :],
            proj[h * CHUNK : (h + 1) * CHUNK, :], NT, preferred_element_type=wider,
        )
        for k in range(2):
            q = (2 * pair + k) * pieces + h
            acc[q] = value[k * height : (k + 1) * height]
            c_send[q] = acc[q, pl.ds(other_row, half), :].astype(low)
            start("B", q, CORE)

    def core_sum(q, offset, size):
        if not isinstance(offset, int):
            offset = pl.multiple_of(offset, PIECE)
        at = pl.multiple_of(core_row + offset, PIECE)
        return acc[q, pl.ds(at, size), :] + c_recv[q, pl.ds(offset, size), :].astype(wider)

    def held(q, offset):
        return acc.at[q, rest_rows(offset, quarter), :]

    def along_z(role, s, q):
        mine, rest = upper * quarter, (1 - upper) * quarter
        if s == 1:
            wait(q, CORE)
            e_send[q] = core_sum(q, 0, half).astype(low)
            start(role, q, INWARD)
        if s == 2:
            wait(q, CORE, INWARD)
            at = pl.ds(pl.multiple_of(rest, quarter), quarter)
            z_send[q] = (core_sum(q, rest, quarter) + e_recv[q, at, :].astype(wider)).astype(low)
            start(role, q, MIDDLE)
            at = pl.ds(pl.multiple_of(mine, quarter), quarter)
            held(q, mine)[...] = core_sum(q, mine, quarter) + e_recv[q, at, :].astype(wider)
        if s == 3:
            wait(q, MIDDLE)
            value = held(q, mine)[...] + z_recv[q].astype(wider)
            x_send[q] = value.astype(low)
            start(role, q, ACROSS)
            held(q, mine)[...] = value
        if s == 4:
            wait(q, ACROSS)
            value = held(q, mine)[...] + x_recv[q].astype(wider)
            full[q, rest_rows(mine, quarter), :] = (value * ace_scale).astype(low)
            start(role, q, SHARE, OUTWARD)
        if s == 5:
            wait(q, SHARE)
            start(role, q, REST, WHOLE)
        if s == 6:
            wait(q, OUTWARD, REST)
            start(role, q, WHOLE)

    def along_x(role, s, q):
        mine, rest = across * quarter, (1 - across) * quarter
        if s == 1:
            wait(q, CORE)
            x_send[q] = core_sum(q, rest, quarter).astype(low)
            start(role, q, ACROSS)
        if s == 2:
            wait(q, ACROSS)
            value = core_sum(q, mine, quarter) + x_recv[q].astype(wider)
            if role == "E":
                e_send[q, :quarter, :] = value.astype(low)
                start(role, q, INWARD)
            else:
                held(q, mine)[...] = value
        if s == 3:
            wait(q, INWARD)
            value = held(q, mine)[...] + e_recv[q, :quarter, :].astype(wider)
            z_send[q] = value.astype(low)
            start(role, q, MIDDLE)
            held(q, mine)[...] = value
        if s == 4:
            wait(q, MIDDLE)
            value = held(q, mine)[...] + z_recv[q].astype(wider)
            full[q, rest_rows(mine, quarter), :] = (value * ace_scale).astype(low)
            start(role, q, OUTWARD, SHARE)
        if s == 5 and role == "E":
            wait(q, OUTWARD)
            start(role, q, SHARE)
        if s == 5 and role == "M":
            wait(q, SHARE)
            start(role, q, WHOLE)
        if s == 6:
            wait(q, SHARE)
            start(role, q, WHOLE)

    def direct(role, s, q):
        if s == 1:
            wait(q, CORE)
            e_send[q] = core_sum(q, 0, half).astype(low)
            start(role, q, 0, 1, 2)
        if s == 2:
            wait(q, 0, 1, 2)
            value = core_sum(q, level * sixteenth, sixteenth)
            for k in range(LEVELS - 1):
                at = slice(k * sixteenth, (k + 1) * sixteenth)
                value = value + e_recv[q, at, :].astype(wider)
            x_send[q, :sixteenth, :] = value.astype(low)
            start(role, q, ACROSS)
            acc[q, rest_rows(level * sixteenth, sixteenth), :] = value
        if s == 3:
            wait(q, ACROSS)
            at = rest_rows(level * sixteenth, sixteenth)
            value = acc[q, at, :] + x_recv[q, :sixteenth, :].astype(wider)
            full[q, at, :] = (value * ace_scale).astype(low)
            start(role, q, 4, 5, 6)
        if s == 4:
            wait(q, 4, 5, 6)
            start(role, q, WHOLE)

    chains = {"z": along_z, "x": along_x, "w": direct}

    def column(ref):
        return jnp.broadcast_to(ref[...].astype(wider), (plane, rows)).T

    def window(g):
        return min(max(g * height - reach, 0), rows - WINDOW)

    def masks():
        begin = column(first)
        end = begin + column(blocks)
        lanes = lax.broadcasted_iota(jnp.int32, (height, TILE), 1).astype(wider)
        for g in range(GROUPS):
            for t in range(WINDOW // TILE):
                ids = jnp.floor((lanes + float(window(g) + t * TILE)) * (1.0 / block))
                keep = (ids >= begin[span(g)]) & (ids < end[span(g)])
                inside[g, t] = jnp.where(keep, 1.0, 0.0)
        energy[...] = column(energies)

    def local_terms(g):
        for p in range(depth):
            cut = resp[span(g), p * plane : (p + 1) * plane]
            unp[span(g), p * plane : (p + 1) * plane] = jnp.dot(
                cut, op_hi[...], preferred_element_type=wider
            ) + jnp.dot(cut, op_lo[...], preferred_element_type=wider)

        @pl.loop(0, height // ROWS)
        def _(i):
            at = pl.ds(pl.multiple_of(g * height + i * ROWS, ROWS), ROWS)
            planes = [resp[at, p * plane : (p + 1) * plane].astype(wider) for p in range(depth)]
            level_of = energy[at, :]
            for p in range(depth):
                cut = slice(p * plane, (p + 1) * plane)
                value = unp[at, cut] + (level_of - pot[cut]) * planes[p]
                value = value - pert[cut] * orb[at, cut].astype(wider)
                for k in range(1, HALO + 1):
                    for q in (p - k, p + k):
                        if 0 <= q < depth:
                            value = value + (KINETIC * COEFFS[k]) * planes[q]
                unp[at, cut] = value

    def halo_terms(g):
        for copy in halos[g]:
            copy.wait_recv()

        @pl.loop(0, height // ROWS)
        def _(i):
            at = pl.ds(pl.multiple_of(g * height + i * ROWS, ROWS), ROWS)
            before = [
                halo_l[at, p * plane : (p + 1) * plane].astype(wider) for p in range(HALO)
            ]
            after = [
                halo_r[at, p * plane : (p + 1) * plane].astype(wider) for p in range(HALO)
            ]
            for p in range(depth):
                value = unp[at, p * plane : (p + 1) * plane]
                for k in range(1, HALO + 1):
                    if p - k < 0:
                        value = value + (KINETIC * COEFFS[k]) * before[HALO + p - k]
                    if p + k >= depth:
                        value = value + (KINETIC * COEFFS[k]) * after[p + k - depth]
                unp[at, p * plane : (p + 1) * plane] = value

    def place(device):
        return pl.ds(pl.multiple_of((device // 2) * PIECE, PIECE), PIECE), device % 2

    def apply(g):
        weights = jnp.concatenate([full[g * pieces + h] for h in range(pieces)], axis=1)
        low_parts = []
        for lo in range(0, cells, WINDOW):
            value = unp[span(g), lo : lo + WINDOW] + jnp.dot(
                weights, proj[:, lo : lo + WINDOW], preferred_element_type=wider
            )
            unp[span(g), lo : lo + WINDOW] = value
            low_parts.append(value.astype(low))
        value = lax.dot_general(
            jnp.concatenate(low_parts, axis=1), orb[window(g) : window(g) + WINDOW, :], NT,
            preferred_element_type=wider,
        )
        for t in range(WINDOW // TILE):
            w_sum[g, t] = value[:, t * TILE : (t + 1) * TILE]
            w_send[g, t] = value[:, t * TILE : (t + 1) * TILE].astype(low)
        for k, device in enumerate(everyone):
            at, t = place(device)
            remote(
                w_send.at[g, t, at, :], w_recv.at[g, k], ws_send.at[g], ws_recv.at[g], device
            ).start()

    def drain(sem, g):
        pltpu.make_async_copy(w_recv.at[g], w_recv.at[g], sem.at[g]).wait()

    def combine(g):
        drain(ws_recv, g)
        at, t = place(me)
        value = w_sum[g, t, at, :]
        for k in range(count - 1):
            value = value + w_recv[g, k].astype(wider)
        w_full[g, t, at, :] = (value * window_scale).astype(low)
        mine = w_full.at[g, t, at, :]
        for device in everyone:
            remote(mine, mine, wg_send.at[g], wg_recv.at[g], device).start()

    outs = []
    for g in range(GROUPS):
        for i, (src, dst) in enumerate(((updated, updated_hbm), (residual, residual_hbm))):
            outs.append(
                pltpu.make_async_copy(src.at[span(g), :], dst.at[span(g), :], out_sem.at[g, i])
            )

    def finish(g):
        drain(wg_recv, g)
        weights = jnp.concatenate(
            [
                (w_full[g, t].astype(wider) * inside[g, t]).astype(low)
                for t in range(WINDOW // TILE)
            ],
            axis=1,
        )
        for lo in range(0, cells, WINDOW):
            at = (span(g), slice(lo, lo + WINDOW))
            value = unp[at] - jnp.dot(
                weights, orb[window(g) : window(g) + WINDOW, lo : lo + WINDOW],
                preferred_element_type=wider,
            )
            residual[at] = value.astype(low)
            updated[at] = (resp[at].astype(wider) + STEP_SIZE * value).astype(low)
        outs[2 * g].start()
        outs[2 * g + 1].start()

    def orbitals_ready():
        loads[1 + pieces].wait()
        masks()

    common = {
        "hs": halo_start, "loc": local_terms, "ht": halo_terms,
        "app": apply, "cmb": combine, "fin": finish,
    }

    def perform(role, name, number):
        if name == "p":
            partials(number // (2 * pieces), number % (2 * pieces))
        elif name == "mask":
            orbitals_ready()
        elif name in common:
            common[name](number)
        elif name == "7":
            wait(number, WHOLE)
        else:
            chains[WAYS[number]](role, int(name), number)

    def sends_done():
        for g in range(GROUPS):
            for copy in halos[g]:
                copy.wait_send()
            drain(ws_send, g)
        for role, condition in (("B", None), ("E", edge), ("M", mid)):
            def body():
                for q, kind in sent[role]:
                    copy_of(q, kind).wait_send()

            if condition is None:
                body()
            else:
                pl.when(condition)(body)

    loads[0].wait()
    pl.semaphore_wait(barrier, count - 1)
    for role, run in itertools.groupby(ORDER[:-1], key=lambda step: step[0]):
        run = list(run)

        def body():
            for step in run:
                perform(*step)

        if role == "B":
            body()
        else:
            pl.when(edge if role == "E" else mid)(body)

    sends_done()
    perform(*ORDER[-1])
    for copy in outs:
        copy.wait()
    for g in range(GROUPS):
        drain(wg_send, g)


def hand_over(updated, residual, updated_out, residual_out, first, second, in_sem, out_sem):
    height = first.shape[0] // GROUPS
    copies = []
    for g in range(GROUPS):
        at = pl.ds(g * height, height)
        for i, (src, held, dst) in enumerate(
            ((updated, first, updated_out), (residual, second, residual_out))
        ):
            copies.append((
                pltpu.make_async_copy(src.at[at, :], held.at[at, :], in_sem.at[g, i]),
                pltpu.make_async_copy(held.at[at, :], dst.at[at, :], out_sem.at[g, i]),
            ))
    for come, _ in copies:
        come.start()
    for come, go in copies:
        come.wait()
        go.start()
    for _, go in copies:
        go.wait()


def shards(
    response, orbitals, projectors, potential, perturbing, energies, window_start, block_count
):
    rows, local = response.shape
    count = lax.axis_size("band")
    cells = local * count
    pieces = projectors.shape[0] // CHUNK
    total = GROUPS * pieces
    height = rows // GROUPS
    half, quarter = height // 2, height // 4
    op = plane_operator()
    op_hi = jnp.asarray(op).astype(jnp.bfloat16)
    op_lo = (jnp.asarray(op) - op_hi.astype(jnp.float32)).astype(jnp.bfloat16)
    low, wider = jnp.bfloat16, jnp.float32
    tiles = WINDOW // TILE
    vmem = pl.BlockSpec(memory_space=pltpu.VMEM)
    hbm = pl.BlockSpec(memory_space=pl.ANY)
    made = pl.pallas_call(
        functools.partial(
            kernel, count,
            1.0 / math.sqrt(cells * projectors.shape[0]), 1.0 / math.sqrt(cells * rows),
        ),
        out_shape=(jax.ShapeDtypeStruct(response.shape, low),) * 2,
        in_specs=[hbm] * 3 + [vmem] * 7,
        out_specs=(hbm, hbm),
        scratch_shapes=[
            pltpu.VMEM(response.shape, low),
            pltpu.VMEM(orbitals.shape, low),
            pltpu.VMEM(projectors.shape, low),
            pltpu.VMEM(response.shape, low),
            pltpu.VMEM(response.shape, low),
            pltpu.VMEM(response.shape, wider),
            pltpu.VMEM((total, height, CHUNK), wider),
            pltpu.VMEM((total, half, CHUNK), low),
            pltpu.VMEM((total, half, CHUNK), low),
            pltpu.VMEM((total, half, CHUNK), low),
            pltpu.VMEM((total, half, CHUNK), low),
            pltpu.VMEM((total, quarter, CHUNK), low),
            pltpu.VMEM((total, quarter, CHUNK), low),
            pltpu.VMEM((total, quarter, CHUNK), low),
            pltpu.VMEM((total, quarter, CHUNK), low),
            pltpu.VMEM((total, height, CHUNK), low),
            pltpu.VMEM((GROUPS, tiles, height, TILE), wider),
            pltpu.VMEM((GROUPS, tiles, height, TILE), low),
            pltpu.VMEM((GROUPS, count - 1, PIECE, TILE), low),
            pltpu.VMEM((GROUPS, tiles, height, TILE), low),
            pltpu.VMEM((GROUPS, tiles, height, TILE), wider),
            pltpu.VMEM((rows, GY * GZ), wider),
            pltpu.VMEM(response.shape, low),
            pltpu.VMEM(response.shape, low),
            pltpu.SemaphoreType.DMA((total, KINDS)),
            pltpu.SemaphoreType.DMA((total, KINDS)),
            pltpu.SemaphoreType.DMA((GROUPS, 2)),
            pltpu.SemaphoreType.DMA((GROUPS, 2)),
            pltpu.SemaphoreType.DMA((pieces + 2,)),
            pltpu.SemaphoreType.DMA((GROUPS,)),
            pltpu.SemaphoreType.DMA((GROUPS,)),
            pltpu.SemaphoreType.DMA((GROUPS,)),
            pltpu.SemaphoreType.DMA((GROUPS,)),
            pltpu.SemaphoreType.DMA((GROUPS, 2)),
        ],
        compiler_params=pltpu.CompilerParams(
            collective_id=0, has_side_effects=True, vmem_limit_bytes=56 * 1024 * 1024
        ),
    )(
        response, orbitals, projectors,
        potential, perturbing,
        energies[None, :], window_start[None, :], block_count[None, :],
        op_hi, op_lo,
    )
    return pl.pallas_call(
        hand_over,
        out_shape=(jax.ShapeDtypeStruct(response.shape, low),) * 2,
        in_specs=[hbm, hbm],
        out_specs=(hbm, hbm),
        scratch_shapes=[pltpu.VMEM(response.shape, low)] * 2
        + [pltpu.SemaphoreType.DMA((GROUPS, 2))] * 2,
        compiler_params=pltpu.CompilerParams(vmem_limit_bytes=60 * 1024 * 1024),
    )(*made)


def solution(mesh):
    fits = mesh.shape["band"] == 4 * LEVELS
    in_specs = (
        P("pert", "band"),
        P(None, "band"),
        P(None, "band"),
        P("band"),
        P(("pert", "band")),
        P(),
        P(),
        P(),
    )
    out_specs = (P("pert", "band"), P("pert", "band"))
    return jax.shard_map(
        shards if fits else plain_shards,
        mesh=mesh, in_specs=in_specs, out_specs=out_specs, check_vma=False,
    )
```
